256 devices in a mesh: dp: 8 (over x_lo, y), member: 8 (over z), mp: 4 (over x_hi, core).
Axes of the slice: x: 4 (x_hi: 2, x_lo: 2; x = x_hi * 2 + x_lo), y: 4, z: 8, core: 2. Of those that a mesh axis runs over, the one named last changes fastest.
Arguments:
- hidden: bfloat16 [1024, 4096], P('dp', ('member', 'mp')), may hold values from -9 to 9
- w_in: bfloat16 [8, 4096, 4096], P('member', 'dp', 'mp'), may hold values from -0.09375 to 0.09375
- w_out: bfloat16 [8, 4096, 4096], P('member', 'mp', 'dp'), may hold values from -0.09375 to 0.09375
- score_vec: float32 [8, 4096], P('member'), may hold values from -1 to 1
- lengths: int32 [8, 4], P('dp'), may hold values from 1 to 64, 128 in all within a row
- reward_offset: int32 [8, 4], P('dp'), may hold values from 0 to 63
- seq_weight: float32 [8, 4], P('dp'), may hold values from -4 to 4
Outputs:
- penalized: float32 [8, 4], P('dp')
- grad_hidden: float32 [1024, 4096], P('dp', ('member', 'mp'))
- grad_in: float32 [8, 4096, 4096], P('member', 'dp', 'mp')
- grad_out: float32 [8, 4096, 4096], P('member', 'mp', 'dp')
The draws below stay inside these ranges and needn't reach their ends.
Inputs may be any that keep to these rules, and one draw needn't show every extreme that they name: Each row of lengths sums to 128, and its largest entry is exactly 64.
All inputs are finite; a program needn't handle non-finite values.
Results may differ from the reference program's by a relative error of at most 0.018.
Values may be sent and summed in bfloat16 or wider, within the bound.
No kernel may reach another device: no remote copies, remote signals or barrier semaphores. Data moves between devices by JAX's collectives and lax.ppermute only.
A program may use at most 64 MiB of HBM per device.

```python
import math
import jax
import jax.numpy as jnp
import numpy as np
from jax import lax

D = 4096
FF = 4096
SLAB = 128
SEQS = 4
MOST = 64
HEADS = 8
SLABS = 8
TOKENS = 1024


def shared_direction(key):
    picks = jax.random.randint(jax.random.fold_in(key, 7101), (D,), 0, 2)
    return (picks * 2 - 1).astype(jnp.float32)


def draw_hidden(key, part):
    direction = shared_direction(key)
    keys = jax.random.split(jax.random.fold_in(key, 7202), 4)
    noise = jnp.clip(jax.random.normal(keys[0], (TOKENS, D), jnp.float32), -4.0, 4.0) * 0.6
    magnitude = jax.random.uniform(keys[1], (TOKENS,), jnp.float32, 0.7, 1.0)
    signs = (jax.random.randint(keys[2], (TOKENS,), 0, 2) * 2 - 1).astype(jnp.float32)
    pairing = jax.random.permutation(keys[3], SLABS)
    slab_of = jnp.arange(TOKENS, dtype=jnp.int32) // SLAB
    block_of = jnp.arange(D, dtype=jnp.int32) // (D // SLABS)
    paired = pairing[slab_of][:, None] == block_of[None, :]
    boost = jnp.where(paired, 3.0, 1.0)
    values = noise * boost + (signs * magnitude)[:, None] * direction[None, :]
    return values.astype(jnp.bfloat16)


def draw_score_vec(key, part):
    direction = shared_direction(key)
    keys = jax.random.split(jax.random.fold_in(key, 7303), 3)
    noise = jnp.clip(jax.random.normal(keys[0], (HEADS, D), jnp.float32), -4.0, 4.0)
    magnitude = jax.random.uniform(keys[1], (HEADS,), jnp.float32, 0.4, 1.0)
    signs = (jax.random.randint(keys[2], (HEADS,), 0, 2) * 2 - 1).astype(jnp.float32)
    values = (signs * magnitude)[:, None] * direction[None, :] + 0.5 * noise
    return (values * (8.0 / D)).astype(jnp.float32)


def touch_ends(drawn, key, smallest, high):
    longest = drawn.shape.index(max(drawn.shape))
    spots = []
    for shift in (0, 1):
        where = [jax.random.randint(jax.random.fold_in(key, axis), (), 0, length) for axis, length in enumerate(drawn.shape)]
        where[longest] = (where[longest] + shift) % drawn.shape[longest]
        spots.append(tuple(where))
    return drawn.at[spots[0]].set(smallest).at[spots[1]].set(high)


def shard_levels(own_key, dims, cuts, low, top_value):
    def one(position, shards_of):
        heights = jax.random.uniform(jax.random.fold_in(jax.random.fold_in(own_key, 6), position), (shards_of,), jnp.float32, low / len(cuts), top_value / len(cuts))
        return jnp.repeat(jnp.exp(heights), dims[position] // shards_of).reshape((-1,) + (1,) * (len(dims) - position - 1))

    loudness = one(*cuts[0])
    for cut in cuts[1:]:
        loudness = loudness * one(*cut)
    return loudness


def length_profile(number_of, total, bound, slope):
    portions = [(1 << 20) // math.isqrt(standing ** slope) + 1 for standing in range(2, number_of + 1)]
    spare, holding = total - bound - (number_of - 1), [1] * (number_of - 1)
    while spare > 0:
        candidates = [i for i in range(number_of - 1) if holding[i] < bound]
        whole, left = sum([portions[i] for i in candidates]), spare
        for i in candidates:
            extra = min(bound - holding[i], max(1, left * portions[i] // whole), spare)
            holding[i] = holding[i] + extra
            spare = spare - extra
    return np.array([bound] + holding)


def uneven_parts(rng, count, total, bound, lean):
    if count == 2:
        one = jax.random.randint(rng, (), max(1, total - bound), min(bound, total - 1) + 1)
        return jnp.stack([one, total - one])
    sizes = jnp.asarray(length_profile(count, total, bound, lean), jnp.int32)
    twos = (count - 1) // 2
    source_of, receiver = sizes[1:1 + 2 * twos:2], sizes[2:2 + 2 * twos:2]
    slack = jnp.minimum(source_of - 1, bound - receiver)
    moved = jax.random.randint(jax.random.fold_in(rng, 1), (twos,), 0, 1 << 20) % (slack + 1)
    sizes = sizes.at[1:1 + 2 * twos:2].set(source_of - moved).at[2:2 + 2 * twos:2].set(receiver + moved)
    return sizes[jax.random.permutation(jax.random.fold_in(rng, 2), count)]


def bell_draw(stream_key, extent, width, most, cuts=(), kind=jnp.bfloat16):
    result = width * jax.random.normal(stream_key, extent, jnp.float32)
    if cuts:
        result = result * shard_levels(stream_key, extent, cuts, -0.22, 0.18)
    return jnp.clip(result, -most, most).astype(kind)


def setup_inputs(seed: int = 0) -> dict:
    arg_keys = jax.random.split(jax.random.key(seed), 8)
    return {
        "hidden": draw_hidden(jax.random.fold_in(arg_keys[7], 71), 0),
        "w_in": bell_draw(arg_keys[1], (HEADS, D, FF), D ** -0.5, 0.09375, ((0, 8), (1, 8), (2, 4))),
        "w_out": bell_draw(arg_keys[2], (HEADS, FF, D), FF ** -0.5, 0.09375, ((0, 8), (1, 4), (2, 8))),
        "score_vec": draw_score_vec(jax.random.fold_in(arg_keys[7], 71), 0),
        "lengths": jax.vmap(lambda own: uneven_parts(own, SEQS, SLAB, MOST, 2))(jax.random.split(arg_keys[4], SLABS)).reshape((SLABS, SEQS)).astype(jnp.int32),
        "reward_offset": touch_ends(jax.random.randint(arg_keys[5], (SLABS, SEQS), 0, MOST), jax.random.fold_in(arg_keys[5], 1), 0, MOST - 1).astype(jnp.int32),
        "seq_weight": bell_draw(arg_keys[6], (SLABS, SEQS), 1.0, 4.0, ((0, 8),), jnp.float32),
    }


PENALTY = 0.5
SPREAD_FLOOR = 0.25
EPSILON = 1e-05
PRECISE = lax.Precision.HIGHEST

def pooling(lengths, offsets, row_count):
    lengths = lengths.astype(jnp.int32)
    seq_ends = jnp.cumsum(lengths).astype(jnp.int32)
    seq_starts = seq_ends - lengths
    target = seq_starts + offsets.astype(jnp.int32) % lengths
    places = jnp.arange(row_count, dtype=jnp.int32)[:, None]
    inside = jnp.logical_and(places >= seq_starts[None, :], places < seq_ends[None, :])
    marked = places == target[None, :]
    return inside.astype(jnp.float32) / lengths.astype(jnp.float32)[None, :] + marked.astype(jnp.float32)

def silu_slope(gate_in):
    sigmoided = jax.nn.sigmoid(gate_in)
    return sigmoided * (1.0 + gate_in * (1.0 - sigmoided))

def slab_forward(slab_rows, w_first, w_second, vector, pooler):
    gate_in = jnp.dot(slab_rows, w_first, preferred_element_type=jnp.float32)
    activated = jax.nn.silu(gate_in).astype(jnp.bfloat16)
    combined = slab_rows.astype(jnp.float32) + jnp.dot(activated, w_second, preferred_element_type=jnp.float32)
    inverse = lax.rsqrt(lax.optimization_barrier(jnp.mean(combined * combined, axis=1)) + EPSILON)
    scores = jnp.dot(combined, vector, precision=PRECISE) * inverse
    rewards = jnp.dot(scores, pooler, precision=PRECISE)
    return (gate_in, activated, combined, inverse, scores, rewards)

def reference(hidden, w_in, w_out, score_vec, lengths, reward_offset, seq_weight):
    slab_count = lengths.shape[0]
    head_count = w_in.shape[0]
    row_count = hidden.shape[0] // slab_count
    feature_count = hidden.shape[1]
    slab_blocks = hidden.reshape(slab_count, row_count, feature_count)
    poolers = jax.vmap(lambda seq_len, seq_off: pooling(seq_len, seq_off, row_count))(lengths, reward_offset)
    head_ids = jnp.arange(head_count, dtype=jnp.int32)

    def forward(head_id):

        def reward_of(entry):
            return slab_forward(entry[0], w_in[head_id], w_out[head_id], score_vec[head_id], entry[1])[5]
        return lax.map(reward_of, (slab_blocks, poolers))
    rewards = lax.map(forward, head_ids)
    center = lax.optimization_barrier(jnp.mean(rewards, axis=0))
    spread = lax.optimization_barrier(jnp.mean((rewards - center) ** 2, axis=0))
    deviation = jnp.sqrt(spread + SPREAD_FLOOR)
    penalized = center - PENALTY * deviation
    seq_pulls = seq_weight[None] * (1.0 - PENALTY * (rewards - center) / deviation) / head_count

    def backward(running, head_id):
        w_first = w_in[head_id]
        w_second = w_out[head_id]
        vector = score_vec[head_id]

        def per_slab(totals, entry):
            slab_rows, pooler, seq_pull = entry
            gate_in, activated, combined, inverse, scores, unused = slab_forward(slab_rows, w_first, w_second, vector, pooler)
            tok_weight = jnp.dot(pooler, seq_pull, precision=PRECISE)
            slopes = tok_weight[:, None] * (vector[None, :] * inverse[:, None] - (scores * inverse * inverse / feature_count)[:, None] * combined)
            slope_half = slopes.astype(jnp.bfloat16)
            back_raw = jnp.dot(slope_half, w_second.T, preferred_element_type=jnp.float32)
            back_gate = (back_raw * silu_slope(gate_in)).astype(jnp.bfloat16)
            hidden_term = slopes + jnp.dot(back_gate, w_first.T, preferred_element_type=jnp.float32)
            part_first = lax.optimization_barrier(jnp.dot(slab_rows.T, back_gate, preferred_element_type=jnp.float32).astype(jnp.bfloat16))
            part_second = lax.optimization_barrier(jnp.dot(activated.T, slope_half, preferred_element_type=jnp.float32).astype(jnp.bfloat16))
            return ((totals[0] + part_first.astype(jnp.float32), totals[1] + part_second.astype(jnp.float32)), hidden_term)
        initial = (jnp.zeros(w_first.shape, jnp.float32), jnp.zeros(w_second.shape, jnp.float32))
        grads_pair, hidden_terms = lax.scan(per_slab, initial, (slab_blocks, poolers, seq_pulls[head_id]))
        return (running + hidden_terms.reshape(slab_count * row_count, feature_count), grads_pair)
    grad_hidden, grads_all = lax.scan(backward, jnp.zeros((slab_count * row_count, feature_count), jnp.float32), head_ids)
    return (penalized, grad_hidden, grads_all[0], grads_all[1])
```

```python
import itertools

import jax
import jax.numpy as jnp
from jax import lax
from jax.sharding import Mesh, PartitionSpec as P

PENALTY = 0.5
SPREAD_FLOOR = 0.25
EPSILON = 1e-05
PRECISE = lax.Precision.HIGHEST
AXES = ("xl", "y", "z", "xh", "c")
SIZES = (2, 4, 8, 2, 2)
BF16 = jnp.bfloat16
F32 = jnp.float32


def permuted(array, axes, target):
    sizes = [SIZES[AXES.index(a)] for a in axes]

    def flat(place):
        index = 0
        for i, size in zip(place, sizes):
            index = index * size + i
        return index

    pairs = [
        (flat(place), flat(target(*place))) for place in itertools.product(*map(range, sizes))
    ]
    return lax.ppermute(array, axes, pairs)


def over_xl(array):
    return permuted(array, ("xl",), lambda xl: (1 - xl,))


def over_xh(array):
    return permuted(array, ("xh",), lambda xh: (1 - xh,))


def over_diagonal(array):
    return permuted(array, ("xl", "xh"), lambda xl, xh: (1 - xl, 1 - xh))


def over_cores(array):
    return permuted(array, ("c",), lambda c: (1 - c,))


def owner_of(xl, y, z, xh, c):
    return (xl, 2 * xh + c, ((z // 4) ^ xl) * 4 + y, (z % 4) // 2, z % 2)


def to_owner(array):
    return permuted(array, AXES, owner_of)


def from_owner(array):
    places = list(itertools.product(*map(range, SIZES)))
    back = {owner_of(*place): place for place in places}
    return permuted(array, AXES, lambda *place: back[place])


def sent_to_all(array, axes):
    count = lax.axis_size(axes)
    return lax.all_to_all(
        jnp.broadcast_to(array[None], (count, *array.shape)), axes, 0, 0, tiled=True
    )


def summed_over_y(partial):
    rows = partial.shape[0] // SIZES[1]
    parts = lax.all_to_all(partial.reshape(SIZES[1], rows, -1), "y", 0, 0, tiled=True)
    return jnp.sum(parts.astype(F32), axis=0)


def gathered_over_y(array):
    return sent_to_all(array, "y").reshape(-1, array.shape[-1])


def mul(left, right):
    return jnp.dot(left, right, preferred_element_type=F32)


def mul_t(left, right):
    return lax.dot_general(left, right, (((1,), (1,)), ((), ())), preferred_element_type=F32)


def t_mul(left, right):
    return lax.dot_general(left, right, (((0,), (0,)), ((), ())), preferred_element_type=F32)


def ring_blocks(block):
    half = block.shape[0] // 2
    by_xl = over_xl(block)
    by_diagonal = over_diagonal(block)
    opposite = (over_xl(by_diagonal[:half]), over_diagonal(by_xl[half:]))
    return block, by_xl, opposite, by_diagonal


def pooling(lengths, offsets, row_count):
    seq_ends = jnp.cumsum(lengths)
    seq_starts = seq_ends - lengths
    target = seq_starts + offsets % lengths
    places = jnp.arange(row_count, dtype=jnp.int32)[:, None]
    inside = jnp.logical_and(places >= seq_starts[None, :], places < seq_ends[None, :])
    marked = places == target[None, :]
    return inside.astype(F32) / lengths.astype(F32)[None, :] + marked.astype(F32)


def silu_slope(gate_in):
    sigmoided = jax.nn.sigmoid(gate_in)
    return sigmoided * (1.0 + gate_in * (1.0 - sigmoided))


def in_three(vector):
    high = vector.astype(BF16)
    rest = vector - high.astype(F32)
    middle = rest.astype(BF16)
    low = (rest - middle.astype(F32)).astype(BF16)
    return jnp.stack([high, middle, low])


def local(hidden, w_in, w_out, score_vec, lengths, reward_offset, seq_weight):
    xl, y, z, xh, c = (lax.axis_index(a) for a in AXES)
    rows, members, features = 128, SIZES[2], 4096
    w_own, w_xl, (w_xh_a, w_xh_b), w_dg = ring_blocks(w_in[0])
    v_start, _ = lax.optimization_barrier((w_out[0], (w_xh_a, w_xh_b)))
    v_own, v_xl, (v_xh_a, v_xh_b), v_dg = ring_blocks(v_start)
    half_in, half_out = w_xh_a.shape[0], v_xh_a.shape[0]
    facts = jnp.concatenate([lengths.astype(F32), reward_offset.astype(F32), seq_weight])
    every_facts = sent_to_all(facts, "y")
    slabs = (2 * xh + c, 2 * xh + 1 - c)
    poolers, pulls = [], []
    for slab in slabs:
        mine = lax.dynamic_index_in_dim(every_facts, slab, 0, keepdims=False)
        poolers.append(pooling(mine[0].astype(jnp.int32), mine[1].astype(jnp.int32), rows))
        pulls.append(mine[2])
    pooler, weight = jnp.stack(poolers), jnp.stack(pulls)
    blocks = sent_to_all(from_owner(hidden), "z").reshape(2, 4, rows, -1)
    slab_mine = jnp.moveaxis(blocks, 1, 2).reshape(2, rows, -1)
    slab_both = jnp.concatenate([slab_mine, over_cores(slab_mine)], axis=1)
    hid_o, hid_t = slab_both[0], slab_both[1]
    part_o = (mul(hid_o, w_own) + mul(hid_t, w_xl)).astype(BF16)
    gate_o = summed_over_y(part_o)
    part_t = (
        mul(hid_o[:, :half_in], w_xh_a) + mul(hid_o[:, half_in:], w_xh_b) + mul(hid_t, w_dg)
    ).astype(BF16)
    gate_t = summed_over_y(part_t)
    gate = jnp.concatenate([gate_o, gate_t], axis=1)
    units = gate_o.shape[1]
    activated = gathered_over_y(jax.nn.silu(gate).astype(BF16))
    act_o, act_t = activated[:, :units], activated[:, units:]
    branch_o = mul(act_o, v_own) + mul(act_t[:, :half_out], v_xh_a) + mul(
        act_t[:, half_out:], v_xh_b
    )
    branch_t = mul(act_o, v_xl) + mul(act_t, v_dg)
    branch = jnp.stack([branch_o, branch_t])
    received = over_cores(branch[:, rows:].astype(BF16))
    combined = slab_mine.astype(F32) + branch[:, :rows] + received.astype(F32)
    width = combined.shape[2]
    vec = jnp.stack(
        [
            lax.dynamic_slice_in_dim(score_vec[0], (4 * xl + y) * width, width),
            lax.dynamic_slice_in_dim(score_vec[0], (4 * (1 - xl) + y) * width, width),
        ]
    )
    combined_half = combined.astype(BF16)
    combined_both = jnp.concatenate([combined_half, over_cores(combined_half)], axis=1)
    sums = jnp.stack(
        [jnp.sum(combined * combined, axis=(0, 2)), jnp.sum(combined * vec[:, None], axis=(0, 2))]
    )
    sums = jnp.stack([sums, over_cores(sums)])
    every = sent_to_all(sums.reshape(4, rows), ("y", "z")).reshape(4, members, 2, 2, rows)
    totals = jnp.sum(every, axis=0)
    inverse = lax.rsqrt(totals[:, :, 0] / features + EPSILON)
    scores = totals[:, :, 1] * inverse
    rewards = jnp.einsum("mot,ots->mos", scores, pooler, precision=PRECISE)
    center = jnp.mean(rewards, axis=0)
    spread = jnp.mean((rewards - center) ** 2, axis=0)
    deviation = jnp.sqrt(spread + SPREAD_FLOOR)
    penalized = center - PENALTY * deviation
    reward, inverse, scores = (
        lax.dynamic_index_in_dim(a, z, 0, keepdims=False) for a in (rewards, inverse, scores)
    )
    seq_pull = weight * (1.0 - PENALTY * (reward - center) / deviation) / members
    tok_weight = jnp.einsum("ots,os->ot", pooler, seq_pull, precision=PRECISE)
    by_vec = (tok_weight * inverse).reshape(-1, 1)
    by_combined = (tok_weight * scores * inverse * inverse / features).reshape(-1, 1)
    by_core = jnp.where(c == 0, penalized, penalized[::-1])
    of_row = jnp.where(y // 2 == xh, by_core, over_xh(by_core))
    reported = lax.dynamic_index_in_dim(of_row, y % 2, 0)
    com_o, com_t = combined_both[0], combined_both[1]
    thirds_o, thirds_t = in_three(vec[0]), in_three(vec[1])

    def against_out(left_o, left_t):
        own = mul_t(left_o, v_own) + mul_t(left_t, v_xl)
        other = jnp.concatenate([mul_t(left_o, v_xh_a), mul_t(left_o, v_xh_b)], axis=1) + mul_t(
            left_t, v_dg
        )
        return jnp.concatenate([own, other], axis=1)

    vec_part = jnp.sum(against_out(thirds_o, thirds_t), axis=0, keepdims=True)
    vec_out = jnp.sum(sent_to_all(vec_part, "y"), axis=0)
    com_out = summed_over_y(against_out(com_o, com_t).astype(BF16))
    piece = com_out.shape[0]
    piece_vec = lax.dynamic_slice_in_dim(by_vec, y * piece, piece, 0)
    piece_com = lax.dynamic_slice_in_dim(by_combined, y * piece, piece, 0)
    back_raw = piece_vec * vec_out - piece_com * com_out
    back_gate = gathered_over_y((back_raw * silu_slope(gate)).astype(BF16))
    back_o, back_t = back_gate[:, :units], back_gate[:, units:]
    back_w_o = mul_t(back_o, w_own) + jnp.concatenate(
        [mul_t(back_t, w_xh_a), mul_t(back_t, w_xh_b)], axis=1
    )
    back_w_t = mul_t(back_o, w_xl) + mul_t(back_t, w_dg)
    back_w = jnp.stack([back_w_o, back_w_t])
    direct = by_vec[:rows] * vec[:, None] - by_combined[:rows] * combined
    term = direct + back_w[:, :rows] + over_cores(back_w[:, rows:].astype(BF16)).astype(F32)
    pieces = jnp.moveaxis(term.astype(BF16).reshape(2, rows, 4, -1), 2, 1).reshape(8, rows, -1)
    from_heads = lax.all_to_all(pieces, "z", 0, 0, tiled=True)
    block = jnp.sum(from_heads.astype(F32), axis=0)
    grad_hidden = to_owner(block.astype(BF16)).astype(F32)
    slopes = (by_vec * vec[:, None] - by_combined * combined_both.astype(F32)).astype(BF16)

    def quarters(own, other):
        return jnp.concatenate([own, over_xl(own), over_xh(other), over_diagonal(other)])

    def feature_quarters(own, other):
        return jnp.concatenate([own, over_xl(other), over_xh(own), over_diagonal(other)])

    grad_out = t_mul(quarters(act_o, act_t), feature_quarters(slopes[0], slopes[1]))
    grad_in = t_mul(feature_quarters(hid_o, hid_t), quarters(back_o, back_t))
    return (reported, grad_hidden, grad_in[None], grad_out[None])


def solution(mesh):
    fine = Mesh(mesh.devices.reshape(SIZES), AXES)
    dp, member, mp = ("xl", "y"), "z", ("xh", "c")
    in_specs = (
        P(dp, (member, *mp)),
        P(member, dp, mp),
        P(member, mp, dp),
        P(member, None),
        P(dp, None),
        P(dp, None),
        P(dp, None),
    )
    out_specs = (
        P(dp, None),
        P(dp, (member, *mp)),
        P(member, dp, mp),
        P(member, mp, dp),
    )
    return jax.shard_map(local, mesh=fine, in_specs=in_specs, out_specs=out_specs, check_vma=False)
```

```python
import functools
import itertools

import jax
import jax.numpy as jnp
from jax import lax
from jax.experimental import pallas as pl
from jax.experimental.pallas import tpu as pltpu
from jax.sharding import Mesh, PartitionSpec as P


PENALTY = 0.5
SPREAD_FLOOR = 0.25
EPSILON = 1e-05
AXES = ("xl", "y", "z", "xh", "c")
SIZES = (2, 4, 8, 2, 2)
BF16 = jnp.bfloat16
F32 = jnp.float32


def permuted(array, axes, target):
    sizes = [SIZES[AXES.index(a)] for a in axes]

    def flat(place):
        index = 0
        for i, size in zip(place, sizes):
            index = index * size + i
        return index

    pairs = [
        (flat(place), flat(target(*place))) for place in itertools.product(*map(range, sizes))
    ]
    return lax.ppermute(array, axes, pairs)


def over_xl(array):
    return permuted(array, ("xl",), lambda xl: (1 - xl,))


def over_xh(array):
    return permuted(array, ("xh",), lambda xh: (1 - xh,))


def over_diagonal(array):
    return permuted(array, ("xl", "xh"), lambda xl, xh: (1 - xl, 1 - xh))


def over_cores(array):
    return permuted(array, ("c",), lambda c: (1 - c,))


def owner_of(xl, y, z, xh, c):
    return (xl, 2 * xh + c, ((z // 4) ^ xl) * 4 + y, (z % 4) // 2, z % 2)


def to_owner(array):
    return permuted(array, AXES, owner_of)


def from_owner(array):
    places = list(itertools.product(*map(range, SIZES)))
    back = {owner_of(*place): place for place in places}
    return permuted(array, AXES, lambda *place: back[place])


def exchanged(array, axes):
    return lax.all_to_all(array, axes, 0, 0, tiled=True)


def sent_to_all(array, axes):
    count = lax.axis_size(axes)
    return exchanged(jnp.broadcast_to(array[None], (count, *array.shape)), axes)


def to_reporter(array):
    return permuted(array, ("y", "xh", "c"), lambda y, xh, c: (2 * xh + c, y // 2, y % 2))


def pieces_over_y(partial):
    return exchanged(partial.reshape(SIZES[1], -1, partial.shape[1]), "y")


def gathered_over_y(copies):
    return exchanged(copies, "y").reshape(-1, copies.shape[-1])


def mul(left, right):
    return jnp.dot(left, right, preferred_element_type=F32)


def mul_t(left, right):
    return lax.dot_general(left, right, (((1,), (1,)), ((), ())), preferred_element_type=F32)


def t_mul(left, right):
    return lax.dot_general(left, right, (((0,), (0,)), ((), ())), preferred_element_type=F32)


def pooling(lengths, offsets, row_count):
    seq_ends = jnp.cumsum(lengths)
    seq_starts = seq_ends - lengths
    target = seq_starts + offsets % lengths
    places = jnp.arange(row_count, dtype=jnp.int32)[:, None]
    inside = jnp.logical_and(places >= seq_starts[None, :], places < seq_ends[None, :])
    marked = places == target[None, :]
    return inside.astype(F32) / lengths.astype(F32)[None, :] + marked.astype(F32)


def silu_slope(gate_in):
    sigmoided = jax.nn.sigmoid(gate_in)
    return sigmoided * (1.0 + gate_in * (1.0 - sigmoided))


VMEM = pl.BlockSpec(memory_space=pltpu.VMEM)
SMEM = pl.BlockSpec(memory_space=pltpu.SMEM)


def limit(mebibytes):
    return pltpu.CompilerParams(vmem_limit_bytes=mebibytes << 20)


def like(shape, dtype):
    return jax.ShapeDtypeStruct(shape, dtype)


def activate_kernel(parts_ref, gate_ref, copies_ref):
    step = 512
    for at in range(0, gate_ref.shape[1], step):
        cols = slice(at, at + step)
        gate = sum(parts_ref[k, :, cols].astype(F32) for k in range(parts_ref.shape[0]))
        gate_ref[:, cols] = gate
        activated = (gate * jax.nn.sigmoid(gate)).astype(BF16)
        for k in range(copies_ref.shape[0]):
            copies_ref[k, :, cols] = activated


def activate(parts):
    count, rows, width = parts.shape
    return pl.pallas_call(
        activate_kernel,
        out_shape=(like((rows, width), F32), like((count, rows, width), BF16)),
        in_specs=[VMEM],
        out_specs=(VMEM, VMEM),
        name="activate",
        compiler_params=limit(6),
    )(parts)


def gate_kernel(mine_ref, partner_ref, own, xl_a, xl_b, dg_a, dg_b, xh_a, xh_b, out_ref):
    half, units = xl_a.shape
    hid_o, hid_t = (jnp.concatenate([mine_ref[i], partner_ref[i]], axis=0) for i in range(2))
    out_ref[:, :units] = (
        mul(hid_o, own[...]) + mul(hid_t[:, :half], xl_a[...]) + mul(hid_t[:, half:], xl_b[...])
    ).astype(BF16)
    out_ref[:, units:] = (
        mul(hid_o[:, :half], xh_a[...])
        + mul(hid_o[:, half:], xh_b[...])
        + mul(hid_t[:, :half], dg_a[...])
        + mul(hid_t[:, half:], dg_b[...])
    ).astype(BF16)


def gate_parts(mine, partner, blocks):
    return pl.pallas_call(
        gate_kernel,
        out_shape=like((2 * mine.shape[1], 2 * blocks[0].shape[1]), BF16),
        in_specs=[VMEM] * 9,
        out_specs=VMEM,
        name="gate",
        compiler_params=limit(14),
    )(mine, partner, *blocks)


def branch_kernel(act_ref, own, xl_a, xl_b, dg_a, dg_b, xh_a, xh_b, away_ref, stay_ref):
    rows, half, units = stay_ref.shape[1], xl_a.shape[0], own.shape[0]
    first = (
        mul(act_ref[:, :units], own[...])
        + mul(act_ref[:, units : units + half], xh_a[...])
        + mul(act_ref[:, units + half :], xh_b[...])
    )
    away_ref[0] = first[rows:].astype(BF16)
    stay_ref[0] = first[:rows]
    second = (
        mul(act_ref[:, :half], xl_a[...])
        + mul(act_ref[:, half:units], xl_b[...])
        + mul(act_ref[:, units : units + half], dg_a[...])
        + mul(act_ref[:, units + half :], dg_b[...])
    )
    away_ref[1] = second[rows:].astype(BF16)
    stay_ref[1] = second[:rows]


def branch_of(act, blocks):
    half, width = act.shape[0] // 2, blocks[0].shape[1]
    return pl.pallas_call(
        branch_kernel,
        out_shape=(like((2, half, width), BF16), like((2, half, width), F32)),
        in_specs=[VMEM] * 8,
        out_specs=(VMEM, VMEM),
        name="branch",
        compiler_params=limit(14),
    )(act, *blocks)


def back_hidden_kernel(back_ref, own, xl_a, xl_b, dg_a, dg_b, xh_a, xh_b, away_ref, stay_ref):
    rows, half, units = stay_ref.shape[1], xl_a.shape[0], own.shape[1]
    back_o, back_t = back_ref[:, :units], back_ref[:, units:]

    def put(i, at, result):
        cols = slice(at, at + result.shape[1])
        away_ref[i, :, cols] = result[rows:].astype(BF16)
        stay_ref[i, :, cols] = result[:rows]

    put(0, 0, mul_t(back_o, own[:half]) + mul_t(back_t, xh_a[...]))
    put(0, half, mul_t(back_o, own[half:]) + mul_t(back_t, xh_b[...]))
    put(1, 0, mul_t(back_o, xl_a[...]) + mul_t(back_t, dg_a[...]))
    put(1, half, mul_t(back_o, xl_b[...]) + mul_t(back_t, dg_b[...]))


def back_hidden(back, blocks):
    half, width = back.shape[0] // 2, blocks[0].shape[0]
    return pl.pallas_call(
        back_hidden_kernel,
        out_shape=(like((2, half, width), BF16), like((2, half, width), F32)),
        in_specs=[VMEM] * 8,
        out_specs=(VMEM, VMEM),
        name="back_hidden",
        compiler_params=limit(14),
    )(back, *blocks)


def as_row(column):
    return jnp.transpose(jnp.broadcast_to(column, (column.shape[0], 128)))[0:1]


def as_columns(row):
    return jnp.transpose(jnp.broadcast_to(row, (128, row.shape[1])))


def combine_kernel(hidden_ref, stay_ref, got_ref, vec_ref, full_ref, half_ref, sums_ref):
    squares = products = 0.0
    for i in range(2):
        combined = hidden_ref[i].astype(F32) + stay_ref[i] + got_ref[i].astype(F32)
        full_ref[i] = combined
        half_ref[i] = combined.astype(BF16)
        squares += jnp.sum(combined * combined, axis=1, keepdims=True)
        products += jnp.sum(combined * vec_ref[i : i + 1], axis=1, keepdims=True)
    sums_ref[0:1] = as_row(squares)
    sums_ref[1:2] = as_row(products)


def combine(hidden, stay, got, vec):
    return pl.pallas_call(
        combine_kernel,
        out_shape=(like(stay.shape, F32), like(stay.shape, BF16), like((2, stay.shape[1]), F32)),
        in_specs=[VMEM] * 4,
        out_specs=(VMEM,) * 3,
        name="combine",
        compiler_params=limit(6),
    )(hidden, stay, got, vec)


def rows_of(values, count):
    width = values[0].shape[1]
    index = lax.broadcasted_iota(jnp.int32, (count, width), 0)
    stacked = jnp.zeros((count, width), F32)
    for i, value in enumerate(values):
        stacked = jnp.where(index == i, jnp.broadcast_to(value, (count, width)), stacked)
    return stacked


def against_kernel(
    place_ref, own_ref, partner_ref, vec_ref, own, xl_a, xl_b, dg_a, dg_b, xh_a, xh_b,
    out_0, out_1, out_2, out_3, both, left,
):
    outs = (out_0, out_1, out_2, out_3)
    rows, half, units = own_ref.shape[1], xl_a.shape[0], own.shape[0]
    piece = 2 * rows // len(outs)
    for i in range(2):
        both[i, :rows] = own_ref[i]
        both[i, rows:] = partner_ref[i]
        for k in range(len(outs)):
            start = pl.multiple_of(((place_ref[0] + k) % len(outs)) * piece, piece)
            left[i, k * piece : (k + 1) * piece] = both[i, pl.ds(start, piece), :]
        vec = vec_ref[i : i + 1]
        high = vec.astype(BF16).astype(F32)
        middle = (vec - high).astype(BF16).astype(F32)
        left[i, 2 * rows :] = rows_of((high, middle, vec - high - middle), 16).astype(BF16)

    def put(result, at):
        vec = jnp.sum(result[2 * rows :], axis=0, keepdims=True)
        high = vec.astype(BF16).astype(F32)
        extra = rows_of((high, vec - high), 8).astype(BF16)
        for k, out in enumerate(outs):
            cols = slice(at, at + result.shape[1])
            out[:piece, cols] = result[k * piece : (k + 1) * piece].astype(BF16)
            out[piece:, cols] = extra

    put(mul_t(left[0], own[:half]) + mul_t(left[1], xl_a[...]), 0)
    put(mul_t(left[0], own[half:]) + mul_t(left[1], xl_b[...]), half)
    put(mul_t(left[0], xh_a[...]) + mul_t(left[1], dg_a[...]), units)
    put(mul_t(left[0], xh_b[...]) + mul_t(left[1], dg_b[...]), units + half)


def against_out(place, own, partner, vec, blocks):
    units, width = blocks[0].shape
    rows = own.shape[1]
    return pl.pallas_call(
        against_kernel,
        out_shape=(like((2 * rows // 4 + 8, 2 * units), BF16),) * 4,
        in_specs=[SMEM] + [VMEM] * 10,
        out_specs=(VMEM,) * 4,
        scratch_shapes=[
            pltpu.VMEM((2, 2 * rows, width), BF16),
            pltpu.VMEM((2, 2 * rows + 16, width), BF16),
        ],
        name="against_out",
        compiler_params=limit(14),
    )(place, own, partner, vec, *blocks)


def back_kernel(
    place_ref, weight_ref, every_ref, pooler_ref, gate_ref, part_0, part_1, part_2, part_3,
    copies_ref, by_vec_ref, by_combined_ref, penalized_ref, *, features,
):
    members, rows = every_ref.shape[1], every_ref.shape[3]
    heads = lax.broadcasted_iota(jnp.int32, (members, 1), 0)
    lanes = lax.broadcasted_iota(jnp.int32, (1, 128), 1)
    mine = heads == place_ref[1]

    def of_mine(values):
        return jnp.sum(jnp.where(mine, values, 0.0), axis=0, keepdims=True)

    penalized = jnp.zeros((1, 128), F32)
    for slab in range(2):
        squares, products = (
            sum(every_ref[k, :, 2 * slab + i, :] for k in range(every_ref.shape[0]))
            for i in range(2)
        )
        inverse = lax.rsqrt(squares / features + EPSILON)
        scores = products * inverse
        tok_weight = jnp.zeros((1, rows), F32)
        for s in range(pooler_ref.shape[1]):
            pool = pooler_ref[slab, s : s + 1, :]
            rewards = jnp.sum(scores * pool, axis=1, keepdims=True)
            center = jnp.sum(rewards, axis=0, keepdims=True) / members
            spread = jnp.sum((rewards - center) ** 2, axis=0, keepdims=True) / members
            deviation = jnp.sqrt(spread + SPREAD_FLOOR)
            if slab == 0:
                penalized = jnp.where(lanes == s, center - PENALTY * deviation, penalized)
            pull = 1.0 - PENALTY * (of_mine(rewards) - center) / deviation
            weight = weight_ref[slab * pooler_ref.shape[1] + s] / members
            tok_weight += weight * pull * pool
        inverse, scores = of_mine(inverse), of_mine(scores)
        at = slice(slab * rows, (slab + 1) * rows)
        by_vec_ref[at] = as_columns(tok_weight * inverse)
        by_combined_ref[at] = as_columns(tok_weight * scores * inverse * inverse / features)
    penalized_ref[...] = penalized
    piece = gate_ref.shape[0]
    start = pl.multiple_of(place_ref[0] * piece, piece)
    by_vec = by_vec_ref[pl.ds(start, piece), 0:1]
    by_combined = by_combined_ref[pl.ds(start, piece), 0:1]
    parts = (part_0, part_1, part_2, part_3)
    step = 512
    for at in range(0, gate_ref.shape[1], step):
        cols = slice(at, at + step)
        combined_out = sum(part[:piece, cols].astype(F32) for part in parts)
        vec_out = jnp.sum(
            sum(part[piece:, cols].astype(F32) for part in parts), axis=0, keepdims=True
        )
        raw = by_vec * vec_out - by_combined * combined_out
        back = (raw * silu_slope(gate_ref[:, cols])).astype(BF16)
        for k in range(copies_ref.shape[0]):
            copies_ref[k, :, cols] = back


def back_of(place, weight, every, pooler, gate, parts, features):
    piece, width = gate.shape
    rows = every.shape[3]
    return pl.pallas_call(
        functools.partial(back_kernel, features=features),
        out_shape=(
            like((4, piece, width), BF16),
            like((2 * rows, 128), F32),
            like((2 * rows, 128), F32),
            like((1, 128), F32),
        ),
        in_specs=[SMEM, SMEM] + [VMEM] * 7,
        out_specs=(VMEM,) * 4,
        name="back",
        compiler_params=limit(8),
    )(place, weight, every, pooler, gate, *parts)


def local(hidden, w_in, w_out, score_vec, lengths, reward_offset, seq_weight):
    xl, y, z, xh, c = (lax.axis_index(a) for a in AXES)
    rows, members, features = 128, SIZES[2], 4096
    mine = from_owner(hidden)

    def ring_blocks(block):
        top, bottom = jnp.split(block, 2)
        dg_a, xl_b = over_diagonal(top), over_xl(bottom)
        xl_a, dg_b = over_xl(top), over_diagonal(bottom)
        xh_a, xh_b = over_xl(dg_a), over_diagonal(xl_b)
        return block, xl_a, xl_b, dg_a, dg_b, xh_a, xh_b

    w_blocks, v_blocks = ring_blocks(w_in[0]), ring_blocks(w_out[0])
    blocks = sent_to_all(mine, "z").reshape(2, 4, rows, -1)
    slab_mine = jnp.moveaxis(blocks, 1, 2).reshape(2, rows, -1)
    slab_partner = over_cores(slab_mine)
    gate, copies = activate(pieces_over_y(gate_parts(slab_mine, slab_partner, w_blocks)))
    units = gate.shape[1] // 2
    activated = gathered_over_y(copies)
    act_o, act_t = activated[:, :units], activated[:, units:]
    facts = jnp.concatenate([lengths.astype(F32), reward_offset.astype(F32), seq_weight])
    turns = [facts] + [
        permuted(facts, ("y",), lambda i, k=k: ((i + k) % SIZES[1],))
        for k in range(1, SIZES[1])
    ]
    turns = jnp.stack(turns)
    poolers, pulls = [], []
    for slab in (2 * xh + c, 2 * xh + 1 - c):
        of_slab = lax.dynamic_index_in_dim(turns, (y - slab) % SIZES[1], 0, keepdims=False)
        poolers.append(pooling(of_slab[0].astype(jnp.int32), of_slab[1].astype(jnp.int32), rows).T)
        pulls.append(of_slab[2])
    pooler, weight = jnp.stack(poolers), jnp.concatenate(pulls)
    width = slab_mine.shape[2]
    vec = jnp.stack(
        [
            lax.dynamic_slice_in_dim(score_vec[0], (4 * xl + y) * width, width),
            lax.dynamic_slice_in_dim(score_vec[0], (4 * (1 - xl) + y) * width, width),
        ]
    )
    away, stay = branch_of(activated, v_blocks)
    combined, combined_half, sums = combine(slab_mine, stay, over_cores(away), vec)
    combined_partner = over_cores(combined_half)
    place = jnp.stack([y, z]).astype(jnp.int32)
    parts = against_out(place, combined_half, combined_partner, vec, v_blocks)
    parts = [parts[0]] + [
        permuted(parts[k], ("y",), lambda i, k=k: ((i + k) % SIZES[1],))
        for k in range(1, SIZES[1])
    ]
    sums = jnp.concatenate([sums, over_cores(sums)])
    every = sent_to_all(sums, ("y", "z")).reshape(SIZES[1], members, 4, rows)
    copies, by_vec, by_combined, penalized = back_of(
        place, weight, every, pooler, gate, parts, features
    )
    by_vec, by_combined = by_vec[:, :1], by_combined[:, :1]
    combined_both = jnp.concatenate([combined_half, combined_partner], axis=1)
    slopes = (by_vec * vec[:, None] - by_combined * combined_both.astype(F32)).astype(BF16)

    def quarters(own, by_xl, by_xh, by_diagonal):
        return (own, over_xl(by_xl), over_xh(by_xh), over_diagonal(by_diagonal))

    act_all = quarters(act_o, act_o, act_t, act_t)
    back_gate = gathered_over_y(copies)
    slope_all = quarters(slopes[0], slopes[1], slopes[0], slopes[1])
    hid_o, hid_t = jnp.concatenate([slab_mine, slab_partner], axis=1)
    hid_all = quarters(hid_o, hid_t, hid_o, hid_t)
    back_o, back_t = back_gate[:, :units], back_gate[:, units:]
    back_all = quarters(back_o, back_o, back_t, back_t)
    away, stay = back_hidden(back_gate, w_blocks)
    direct = by_vec[:rows] * vec[:, None] - by_combined[:rows] * combined
    term = direct + stay + over_cores(away).astype(F32)
    parts = jnp.moveaxis(term.astype(BF16).reshape(2, rows, 4, -1), 2, 1).reshape(8, rows, -1)
    from_heads = exchanged(parts, "z")
    block = jnp.sum(from_heads.astype(F32), axis=0)
    grad_hidden = to_owner(block.astype(BF16)).astype(F32)
    reported = to_reporter(penalized[:, : lengths.shape[1]])
    grad_out = t_mul(jnp.concatenate(act_all), jnp.concatenate(slope_all))
    grad_in = t_mul(jnp.concatenate(hid_all), jnp.concatenate(back_all))
    return (reported, grad_hidden, grad_in[None], grad_out[None])


def solution(mesh):
    fine = Mesh(mesh.devices.reshape(SIZES), AXES)
    dp, member, mp = ("xl", "y"), "z", ("xh", "c")
    in_specs = (
        P(dp, (member, *mp)),
        P(member, dp, mp),
        P(member, mp, dp),
        P(member, None),
        P(dp, None),
        P(dp, None),
        P(dp, None),
    )
    out_specs = (
        P(dp, None),
        P(dp, (member, *mp)),
        P(member, dp, mp),
        P(member, mp, dp),
    )
    return jax.shard_map(local, mesh=fine, in_specs=in_specs, out_specs=out_specs, check_vma=False)
```

```python
import functools
import itertools

import jax
import jax.numpy as jnp
from jax import lax
from jax.experimental import pallas as pl
from jax.experimental.pallas import tpu as pltpu
from jax.sharding import Mesh, PartitionSpec as P


PENALTY = 0.5
SPREAD_FLOOR = 0.25
EPSILON = 1e-05
AXES = ("xl", "y", "z", "xh", "c")
SIZES = (2, 4, 8, 2, 2)
BF16 = jnp.bfloat16
F32 = jnp.float32


def permuted(array, axes, target):
    sizes = [SIZES[AXES.index(a)] for a in axes]

    def flat(place):
        index = 0
        for i, size in zip(place, sizes):
            index = index * size + i
        return index

    pairs = [
        (flat(place), flat(target(*place))) for place in itertools.product(*map(range, sizes))
    ]
    return lax.ppermute(array, axes, pairs)


def over_xl(array):
    return permuted(array, ("xl",), lambda xl: (1 - xl,))


def over_xh(array):
    return permuted(array, ("xh",), lambda xh: (1 - xh,))


def over_diagonal(array):
    return permuted(array, ("xl", "xh"), lambda xl, xh: (1 - xl, 1 - xh))


def over_cores(array):
    return permuted(array, ("c",), lambda c: (1 - c,))


def owner_of(xl, y, z, xh, c):
    return (xl, 2 * xh + c, ((z // 4) ^ xl) * 4 + y, (z % 4) // 2, z % 2)


def to_owner(array):
    return permuted(array, AXES, owner_of)


def from_owner(array):
    places = list(itertools.product(*map(range, SIZES)))
    back = {owner_of(*place): place for place in places}
    return permuted(array, AXES, lambda *place: back[place])


def exchanged(array, axes):
    return lax.all_to_all(array, axes, 0, 0, tiled=True)


def sent_to_all(array, axes):
    count = lax.axis_size(axes)
    return exchanged(jnp.broadcast_to(array[None], (count, *array.shape)), axes)


def to_reporter(array):
    return permuted(array, ("y", "xh", "c"), lambda y, xh, c: (2 * xh + c, y // 2, y % 2))


def pieces_over_y(partial):
    return exchanged(partial.reshape(SIZES[1], -1, partial.shape[1]), "y")


def gathered_over_y(copies):
    return exchanged(copies, "y").reshape(-1, copies.shape[-1])


def mul(left, right):
    return jnp.dot(left, right, preferred_element_type=F32)


def mul_t(left, right):
    return lax.dot_general(left, right, (((1,), (1,)), ((), ())), preferred_element_type=F32)


def t_mul(left, right):
    return lax.dot_general(left, right, (((0,), (0,)), ((), ())), preferred_element_type=F32)


def pooling(lengths, offsets, row_count):
    seq_ends = jnp.cumsum(lengths)
    seq_starts = seq_ends - lengths
    target = seq_starts + offsets % lengths
    places = jnp.arange(row_count, dtype=jnp.int32)[:, None]
    inside = jnp.logical_and(places >= seq_starts[None, :], places < seq_ends[None, :])
    marked = places == target[None, :]
    return inside.astype(F32) / lengths.astype(F32)[None, :] + marked.astype(F32)


def silu_slope(gate_in):
    sigmoided = jax.nn.sigmoid(gate_in)
    return sigmoided * (1.0 + gate_in * (1.0 - sigmoided))


VMEM = pl.BlockSpec(memory_space=pltpu.VMEM)
SMEM = pl.BlockSpec(memory_space=pltpu.SMEM)


def limit(mebibytes):
    return pltpu.CompilerParams(vmem_limit_bytes=mebibytes << 20)


def like(shape, dtype):
    return jax.ShapeDtypeStruct(shape, dtype)


def activate_kernel(parts_ref, gate_ref, copies_ref):
    step = 512
    for at in range(0, gate_ref.shape[1], step):
        cols = slice(at, at + step)
        gate = sum(parts_ref[k, :, cols].astype(F32) for k in range(parts_ref.shape[0]))
        gate_ref[:, cols] = gate
        activated = (gate * jax.nn.sigmoid(gate)).astype(BF16)
        for k in range(copies_ref.shape[0]):
            copies_ref[k, :, cols] = activated


def activate(parts):
    count, rows, width = parts.shape
    return pl.pallas_call(
        activate_kernel,
        out_shape=(like((rows, width), F32), like((count, rows, width), BF16)),
        in_specs=[VMEM],
        out_specs=(VMEM, VMEM),
        name="activate",
        compiler_params=limit(6),
    )(parts)


def gate_kernel(mine_ref, partner_ref, own, xl_a, xl_b, dg_a, dg_b, xh_a, xh_b, out_ref):
    half, units = xl_a.shape
    hid_o, hid_t = (jnp.concatenate([mine_ref[i], partner_ref[i]], axis=0) for i in range(2))
    out_ref[:, :units] = (
        mul(hid_o, own[...]) + mul(hid_t[:, :half], xl_a[...]) + mul(hid_t[:, half:], xl_b[...])
    ).astype(BF16)
    out_ref[:, units:] = (
        mul(hid_o[:, :half], xh_a[...])
        + mul(hid_o[:, half:], xh_b[...])
        + mul(hid_t[:, :half], dg_a[...])
        + mul(hid_t[:, half:], dg_b[...])
    ).astype(BF16)


def gate_parts(mine, partner, blocks):
    return pl.pallas_call(
        gate_kernel,
        out_shape=like((2 * mine.shape[1], 2 * blocks[0].shape[1]), BF16),
        in_specs=[VMEM] * 9,
        out_specs=VMEM,
        name="gate",
        compiler_params=limit(14),
    )(mine, partner, *blocks)


def branch_kernel(act_ref, own, xl_a, xl_b, dg_a, dg_b, xh_a, xh_b, away_ref, stay_ref):
    rows, half, units = stay_ref.shape[1], xl_a.shape[0], own.shape[0]
    first = (
        mul(act_ref[:, :units], own[...])
        + mul(act_ref[:, units : units + half], xh_a[...])
        + mul(act_ref[:, units + half :], xh_b[...])
    )
    away_ref[0] = first[rows:].astype(BF16)
    stay_ref[0] = first[:rows]
    second = (
        mul(act_ref[:, :half], xl_a[...])
        + mul(act_ref[:, half:units], xl_b[...])
        + mul(act_ref[:, units : units + half], dg_a[...])
        + mul(act_ref[:, units + half :], dg_b[...])
    )
    away_ref[1] = second[rows:].astype(BF16)
    stay_ref[1] = second[:rows]


def branch_of(act, blocks):
    half, width = act.shape[0] // 2, blocks[0].shape[1]
    return pl.pallas_call(
        branch_kernel,
        out_shape=(like((2, half, width), BF16), like((2, half, width), F32)),
        in_specs=[VMEM] * 8,
        out_specs=(VMEM, VMEM),
        name="branch",
        compiler_params=limit(14),
    )(act, *blocks)


def back_hidden_kernel(back_ref, own, xl_a, xl_b, dg_a, dg_b, xh_a, xh_b, away_ref, stay_ref):
    rows, half, units = stay_ref.shape[1], xl_a.shape[0], own.shape[1]
    back_o, back_t = back_ref[:, :units], back_ref[:, units:]

    def put(i, at, result):
        cols = slice(at, at + result.shape[1])
        away_ref[i, :, cols] = result[rows:].astype(BF16)
        stay_ref[i, :, cols] = result[:rows]

    put(0, 0, mul_t(back_o, own[:half]) + mul_t(back_t, xh_a[...]))
    put(0, half, mul_t(back_o, own[half:]) + mul_t(back_t, xh_b[...]))
    put(1, 0, mul_t(back_o, xl_a[...]) + mul_t(back_t, dg_a[...]))
    put(1, half, mul_t(back_o, xl_b[...]) + mul_t(back_t, dg_b[...]))


def back_hidden(back, blocks):
    half, width = back.shape[0] // 2, blocks[0].shape[0]
    return pl.pallas_call(
        back_hidden_kernel,
        out_shape=(like((2, half, width), BF16), like((2, half, width), F32)),
        in_specs=[VMEM] * 8,
        out_specs=(VMEM, VMEM),
        name="back_hidden",
        compiler_params=limit(14),
    )(back, *blocks)


def as_row(column):
    return jnp.transpose(jnp.broadcast_to(column, (column.shape[0], 128)))[0:1]


def as_columns(row):
    return jnp.transpose(jnp.broadcast_to(row, (128, row.shape[1])))


def combine_kernel(hidden_ref, stay_ref, got_ref, vec_ref, half_ref, sums_ref):
    squares = products = 0.0
    for i in range(2):
        combined = hidden_ref[i].astype(F32) + stay_ref[i] + got_ref[i].astype(F32)
        half_ref[i] = combined.astype(BF16)
        squares += jnp.sum(combined * combined, axis=1, keepdims=True)
        products += jnp.sum(combined * vec_ref[i : i + 1], axis=1, keepdims=True)
    sums_ref[0:1] = as_row(squares)
    sums_ref[1:2] = as_row(products)


def combine(hidden, stay, got, vec):
    return pl.pallas_call(
        combine_kernel,
        out_shape=(like(stay.shape, BF16), like((2, stay.shape[1]), F32)),
        in_specs=[VMEM] * 4,
        out_specs=(VMEM,) * 2,
        name="combine",
        compiler_params=limit(6),
    )(hidden, stay, got, vec)


def rows_of(values, count):
    width = values[0].shape[1]
    index = lax.broadcasted_iota(jnp.int32, (count, width), 0)
    stacked = jnp.zeros((count, width), F32)
    for i, value in enumerate(values):
        stacked = jnp.where(index == i, jnp.broadcast_to(value, (count, width)), stacked)
    return stacked


def against_kernel(
    place_ref, own_ref, partner_ref, vec_ref, own, xl_a, xl_b, dg_a, dg_b, xh_a, xh_b,
    out_0, out_1, out_2, out_3, both, left,
):
    outs = (out_0, out_1, out_2, out_3)
    rows, half, units = own_ref.shape[1], xl_a.shape[0], own.shape[0]
    piece = 2 * rows // len(outs)
    for i in range(2):
        both[i, :rows] = own_ref[i]
        both[i, rows:] = partner_ref[i]
        for k in range(len(outs)):
            start = pl.multiple_of(((place_ref[0] + k) % len(outs)) * piece, piece)
            left[i, k * piece : (k + 1) * piece] = both[i, pl.ds(start, piece), :]
        vec = vec_ref[i : i + 1]
        high = vec.astype(BF16).astype(F32)
        middle = (vec - high).astype(BF16).astype(F32)
        left[i, 2 * rows :] = rows_of((high, middle, vec - high - middle), 16).astype(BF16)

    def put(result, at):
        vec = jnp.sum(result[2 * rows :], axis=0, keepdims=True)
        high = vec.astype(BF16).astype(F32)
        extra = rows_of((high, vec - high), 8).astype(BF16)
        for k, out in enumerate(outs):
            cols = slice(at, at + result.shape[1])
            out[:piece, cols] = result[k * piece : (k + 1) * piece].astype(BF16)
            out[piece:, cols] = extra

    put(mul_t(left[0], own[:half]) + mul_t(left[1], xl_a[...]), 0)
    put(mul_t(left[0], own[half:]) + mul_t(left[1], xl_b[...]), half)
    put(mul_t(left[0], xh_a[...]) + mul_t(left[1], dg_a[...]), units)
    put(mul_t(left[0], xh_b[...]) + mul_t(left[1], dg_b[...]), units + half)


def against_out(place, own, partner, vec, blocks):
    units, width = blocks[0].shape
    rows = own.shape[1]
    return pl.pallas_call(
        against_kernel,
        out_shape=(like((2 * rows // 4 + 8, 2 * units), BF16),) * 4,
        in_specs=[SMEM] + [VMEM] * 10,
        out_specs=(VMEM,) * 4,
        scratch_shapes=[
            pltpu.VMEM((2, 2 * rows, width), BF16),
            pltpu.VMEM((2, 2 * rows + 16, width), BF16),
        ],
        name="against_out",
        compiler_params=limit(14),
    )(place, own, partner, vec, *blocks)


def token_kernel(
    place_ref, weight_ref, every_ref, pooler_ref,
    by_vec_ref, by_combined_ref, piece_vec_ref, piece_combined_ref, penalized_ref, *, features,
):
    members, rows = every_ref.shape[1], every_ref.shape[3]
    heads = lax.broadcasted_iota(jnp.int32, (members, 1), 0)
    lanes = lax.broadcasted_iota(jnp.int32, (1, 128), 1)
    mine = heads == place_ref[1]

    def of_mine(values):
        return jnp.sum(jnp.where(mine, values, 0.0), axis=0, keepdims=True)

    penalized = jnp.zeros((1, 128), F32)
    for slab in range(2):
        squares, products = (
            sum(every_ref[k, :, 2 * slab + i, :] for k in range(every_ref.shape[0]))
            for i in range(2)
        )
        inverse = lax.rsqrt(squares / features + EPSILON)
        scores = products * inverse
        tok_weight = jnp.zeros((1, rows), F32)
        for s in range(pooler_ref.shape[1]):
            pool = pooler_ref[slab, s : s + 1, :]
            rewards = jnp.sum(scores * pool, axis=1, keepdims=True)
            center = jnp.sum(rewards, axis=0, keepdims=True) / members
            spread = jnp.sum((rewards - center) ** 2, axis=0, keepdims=True) / members
            deviation = jnp.sqrt(spread + SPREAD_FLOOR)
            if slab == 0:
                penalized = jnp.where(lanes == s, center - PENALTY * deviation, penalized)
            pull = 1.0 - PENALTY * (of_mine(rewards) - center) / deviation
            weight = weight_ref[slab * pooler_ref.shape[1] + s] / members
            tok_weight += weight * pull * pool
        inverse, scores = of_mine(inverse), of_mine(scores)
        at = slice(slab * rows, (slab + 1) * rows)
        by_vec_ref[at] = as_columns(tok_weight * inverse)
        by_combined_ref[at] = as_columns(tok_weight * scores * inverse * inverse / features)
    penalized_ref[...] = penalized
    piece = piece_vec_ref.shape[0]
    start = pl.multiple_of(place_ref[0] * piece, piece)
    piece_vec_ref[...] = by_vec_ref[pl.ds(start, piece), :]
    piece_combined_ref[...] = by_combined_ref[pl.ds(start, piece), :]


def token_factors(place, weight, every, pooler, piece, features):
    rows = every.shape[3]
    return pl.pallas_call(
        functools.partial(token_kernel, features=features),
        out_shape=(like((2 * rows, 128), F32),) * 2
        + (like((piece, 128), F32),) * 2
        + (like((1, 128), F32),),
        in_specs=[SMEM, SMEM, VMEM, VMEM],
        out_specs=(VMEM,) * 5,
        name="tokens",
        compiler_params=limit(4),
    )(place, weight, every, pooler)


def local(hidden, w_in, w_out, score_vec, lengths, reward_offset, seq_weight):
    xl, y, z, xh, c = (lax.axis_index(a) for a in AXES)
    rows, members, features = 128, SIZES[2], 4096
    mine = from_owner(hidden)

    def ring_blocks(block):
        top, bottom = jnp.split(block, 2)
        dg_a, xl_b = over_diagonal(top), over_xl(bottom)
        xl_a, dg_b = over_xl(top), over_diagonal(bottom)
        xh_a, xh_b = over_xl(dg_a), over_diagonal(xl_b)
        return block, xl_a, xl_b, dg_a, dg_b, xh_a, xh_b

    w_blocks, v_blocks = ring_blocks(w_in[0]), ring_blocks(w_out[0])
    blocks = sent_to_all(mine, "z").reshape(2, 4, rows, -1)
    slab_mine = jnp.moveaxis(blocks, 1, 2).reshape(2, rows, -1)
    slab_partner = over_cores(slab_mine)
    gate, copies = activate(pieces_over_y(gate_parts(slab_mine, slab_partner, w_blocks)))
    units = gate.shape[1] // 2
    activated = gathered_over_y(copies)
    act_o, act_t = activated[:, :units], activated[:, units:]
    facts = jnp.concatenate([lengths.astype(F32), reward_offset.astype(F32), seq_weight])
    turns = [facts] + [
        permuted(facts, ("y",), lambda i, k=k: ((i + k) % SIZES[1],))
        for k in range(1, SIZES[1])
    ]
    turns = jnp.stack(turns)
    poolers, pulls = [], []
    for slab in (2 * xh + c, 2 * xh + 1 - c):
        of_slab = lax.dynamic_index_in_dim(turns, (y - slab) % SIZES[1], 0, keepdims=False)
        poolers.append(pooling(of_slab[0].astype(jnp.int32), of_slab[1].astype(jnp.int32), rows).T)
        pulls.append(of_slab[2])
    pooler, weight = jnp.stack(poolers), jnp.concatenate(pulls)
    width = slab_mine.shape[2]
    vec = jnp.stack(
        [
            lax.dynamic_slice_in_dim(score_vec[0], (4 * xl + y) * width, width),
            lax.dynamic_slice_in_dim(score_vec[0], (4 * (1 - xl) + y) * width, width),
        ]
    )
    away, stay = branch_of(activated, v_blocks)
    combined_half, sums = combine(slab_mine, stay, over_cores(away), vec)
    combined_partner = over_cores(combined_half)
    place = jnp.stack([y, z]).astype(jnp.int32)
    parts = against_out(place, combined_half, combined_partner, vec, v_blocks)
    parts = [parts[0]] + [
        permuted(parts[k], ("y",), lambda i, k=k: ((i + k) % SIZES[1],))
        for k in range(1, SIZES[1])
    ]
    sums = jnp.concatenate([sums, over_cores(sums)])
    every = sent_to_all(sums, ("y", "z")).reshape(SIZES[1], members, 4, rows)
    piece = gate.shape[0]
    *factors, penalized = token_factors(place, weight, every, pooler, piece, features)
    by_vec, by_combined, piece_vec, piece_combined = (factor[:, :1] for factor in factors)
    of_y = sum(part.astype(F32) for part in parts)
    vec_out = jnp.sum(of_y[piece:], axis=0, keepdims=True)
    back_raw = piece_vec * vec_out - piece_combined * of_y[:piece]
    back_piece = (back_raw * silu_slope(gate)).astype(BF16)
    combined_both = jnp.concatenate([combined_half, combined_partner], axis=1)
    slopes = (by_vec * vec[:, None] - by_combined * combined_both.astype(F32)).astype(BF16)

    def quarters(own, by_xl, by_xh, by_diagonal):
        return (own, over_xl(by_xl), over_xh(by_xh), over_diagonal(by_diagonal))

    act_all = quarters(act_o, act_o, act_t, act_t)
    back_gate = sent_to_all(back_piece, "y").reshape(2 * rows, -1)
    slope_all = quarters(slopes[0], slopes[1], slopes[0], slopes[1])
    hid_o, hid_t = jnp.concatenate([slab_mine, slab_partner], axis=1)
    hid_all = quarters(hid_o, hid_t, hid_o, hid_t)
    back_o, back_t = back_gate[:, :units], back_gate[:, units:]
    back_all = quarters(back_o, back_o, back_t, back_t)
    away, stay = back_hidden(back_gate, w_blocks)
    direct = by_vec[:rows] * vec[:, None] - by_combined[:rows] * combined_half.astype(F32)
    term = direct + stay + over_cores(away).astype(F32)
    parts = jnp.moveaxis(term.astype(BF16).reshape(2, rows, 4, -1), 2, 1).reshape(8, rows, -1)
    from_heads = exchanged(parts, "z")
    block = jnp.sum(from_heads.astype(F32), axis=0)
    grad_hidden = to_owner(block.astype(BF16)).astype(F32)
    reported = to_reporter(penalized[:, : lengths.shape[1]])
    grad_out = t_mul(jnp.concatenate(act_all), jnp.concatenate(slope_all))
    grad_in = t_mul(jnp.concatenate(hid_all), jnp.concatenate(back_all))
    return (reported, grad_hidden, grad_in[None], grad_out[None])


def solution(mesh):
    fine = Mesh(mesh.devices.reshape(SIZES), AXES)
    dp, member, mp = ("xl", "y"), "z", ("xh", "c")
    in_specs = (
        P(dp, (member, *mp)),
        P(member, dp, mp),
        P(member, mp, dp),
        P(member, None),
        P(dp, None),
        P(dp, None),
        P(dp, None),
    )
    out_specs = (
        P(dp, None),
        P(dp, (member, *mp)),
        P(member, dp, mp),
        P(member, mp, dp),
    )
    return jax.shard_map(local, mesh=fine, in_specs=in_specs, out_specs=out_specs, check_vma=False)
```
